256 devices in a mesh: seq: 64 (over x, z, core), head: 4 (over y).
Axes of the slice: x: 4, y: 4, z: 8, core: 2. Of those that a mesh axis runs over, the one named last changes fastest.
Arguments:
- values: float32 [16384, 2560], P('seq', 'head'), may hold values from -6 to 6
- input_map: float32 [16384, 128], P('seq'), may hold values from -6 to 6
- output_map: float32 [16384, 128], P('seq'), may hold values from -6 to 6
- step_sizes: float32 [40, 16384], P('head', 'seq'), may hold values from 0.004 to 0.02
- decay_rates: float32 [40], P('head'), may hold values from 0.02 to 2
- skip_gains: float32 [40], P('head'), may hold values from 0.5 to 1.5
- doc_lengths: int32 [128], replicated, may hold values from 1 to 1024, 16384 in all
- out_grad: float32 [16384, 2560], P('seq', 'head'), may hold values from -6 to 6
Outputs:
- outputs: bfloat16 [16384, 2560], P('seq', 'head')
- grad_values: bfloat16 [16384, 2560], P('seq', 'head')
- grad_input_map: float32 [16384, 128], P('seq')
- grad_output_map: float32 [16384, 128], P('seq')
The draws below stay inside these ranges and needn't reach their ends.
Inputs may be any that keep to these rules, and one draw needn't show every extreme that they name: `doc_lengths`: the documents fill the stream of 16384 tokens in order; no document has more than 1024 tokens, and one has exactly that many.
All inputs are finite; a program needn't handle non-finite values.
Results may differ from the reference program's by a relative error of at most 0.001.
Values sent between devices are 32-bit elements; how exact they have to be, the bound alone decides.
No kernel may reach another device: no remote copies, remote signals or barrier semaphores. Data moves between devices by JAX's collectives and lax.ppermute only.
A program may use at most 128 MiB of HBM per device.

```python
import math
import jax
import jax.numpy as jnp
import numpy as np
from jax import lax

HEAD_SIZE = 64
STATE = 128
HEADS = 40
GROUP = 256
DOC_SPAN = 4
TOK_DEV = 256
TOKENS = 16384
NDOCS = 128


def shard_levels(own_key, dims, cuts, low, high):
    loudness = 1.0
    for axis_at, parts in cuts:
        steps = jax.random.uniform(jax.random.fold_in(jax.random.fold_in(own_key, 6), axis_at), (parts,), jnp.float32, low / len(cuts), high / len(cuts))
        loudness = loudness * jnp.repeat(jnp.exp(steps), dims[axis_at] // parts).reshape((-1,) + (1,) * (len(dims) - 1 - axis_at))
    return loudness


def split_up(count, total, reach, slope):
    portions = [(1 << 20) // math.isqrt(rank ** slope) + 1 for rank in range(2, count + 1)]
    spare, counts = total - reach - (count - 1), [1] * (count - 1)
    while spare > 0:
        movable = [i for i in range(count - 1) if counts[i] < reach]
        mass, remaining = sum([portions[i] for i in movable]), spare
        for i in movable:
            more = min(reach - counts[i], max(1, remaining * portions[i] // mass), spare)
            counts[i] = counts[i] + more
            spare = spare - more
    return np.array([reach] + counts)


def ragged_sizes(stream_key, number_of, total, limit, skew):
    if number_of == 2:
        one = jax.random.randint(stream_key, (), max(1, total - limit), min(limit, total - 1) + 1)
        return jnp.stack([one, total - one])
    sizes = jnp.asarray(split_up(number_of, total, limit, skew), jnp.int32)
    pairs = (number_of - 1) // 2
    source_of, receiver = sizes[1:1 + 2 * pairs:2], sizes[2:2 + 2 * pairs:2]
    room = jnp.minimum(source_of - 1, limit - receiver)
    passed = jax.random.randint(jax.random.fold_in(stream_key, 1), (pairs,), 0, 1 << 20) % (room + 1)
    sizes = sizes.at[1:1 + 2 * pairs:2].set(source_of - passed).at[2:2 + 2 * pairs:2].set(receiver + passed)
    return sizes[jax.random.permutation(jax.random.fold_in(stream_key, 2), number_of)]


def centred(key, extent, deviation, reach, shards=(), held_as=jnp.bfloat16):
    values = jax.random.normal(key, extent, jnp.float32) * deviation
    if len(shards) > 0:
        values = shard_levels(key, extent, shards, -0.22, 0.18) * values
    return jnp.clip(values, min=-reach, max=reach).astype(held_as)


def setup_inputs(seed: int = 0) -> dict:
    arg_keys = jax.random.split(jax.random.key(seed), 9)
    values = centred(arg_keys[0], (TOKENS, HEADS * HEAD_SIZE), 1.0, 6.0, ((0, 64), (1, 4)), jnp.float32)
    input_map = centred(arg_keys[1], (TOKENS, STATE), 1.0, 6.0, ((0, 64),), jnp.float32)
    output_map = centred(arg_keys[2], (TOKENS, STATE), 1.0, 6.0, ((0, 64),), jnp.float32)
    step_sizes = jnp.clip(jnp.exp(math.log(0.02) - 1.6094378 * jax.random.uniform(arg_keys[3], (HEADS, TOKENS), jnp.float32) ** shard_levels(arg_keys[3], (HEADS, TOKENS), ((0, 4), (1, 64)), -0.2, 0.2)), 0.004, 0.02)
    decay_rates = jnp.clip(jnp.exp(math.log(2.0) - 4.6051702 * jax.random.uniform(arg_keys[4], (HEADS,), jnp.float32) ** shard_levels(arg_keys[4], (HEADS,), ((0, 4),), -0.2, 0.2)), 0.02, 2.0)
    skip_gains = jnp.clip(0.5 + 1.0 * jax.random.uniform(arg_keys[5], (HEADS,), jnp.float32) ** shard_levels(arg_keys[5], (HEADS,), ((0, 4),), -0.2, 0.2), 0.5, 1.5)
    doc_lengths = ragged_sizes(arg_keys[6], NDOCS, TOKENS, DOC_SPAN * TOK_DEV, 2).astype(jnp.int32)
    out_grad = centred(arg_keys[7], (TOKENS, HEADS * HEAD_SIZE), 1.0, 6.0, ((0, 64), (1, 4)), jnp.float32)
    return {"values": values, "input_map": input_map, "output_map": output_map, "step_sizes": step_sizes, "decay_rates": decay_rates, "skip_gains": skip_gains, "doc_lengths": doc_lengths, "out_grad": out_grad}


highest = lax.Precision.HIGHEST


def edge_decays(log_decay, restart):
    running = jnp.cumsum(log_decay, axis=1)
    resets_seen = jnp.cumsum(restart)
    inward = jnp.where(resets_seen[None, :] == 0, jnp.exp(running), 0.0)
    outward = jnp.where(resets_seen[None, :] == resets_seen[-1], jnp.exp(running[:, -1:] - running), 0.0)
    whole_decay = jnp.where(resets_seen[-1] == 0, jnp.exp(running[:, -1]), 0.0)
    return running, resets_seen, inward, outward, whole_decay


def group_pass(values, bmat, cmat, steps, rates, skips, restart, grad_y):
    length, head_count, head_width = values.shape
    blocks = length // GROUP
    log_decay = -rates[:, None] * steps

    def blocked(array):
        return array.reshape((blocks, GROUP) + array.shape[1:])

    def blocked_heads(array):
        return jnp.transpose(array.reshape(head_count, blocks, GROUP), (1, 0, 2))

    grouped = (blocked(values), blocked(grad_y), blocked(bmat), blocked(cmat), blocked_heads(steps), blocked_heads(log_decay), blocked(restart))
    causal = jnp.arange(GROUP)[:, None] >= jnp.arange(GROUP)[None, :]

    def forward(carry_state, item):
        piece_x, piece_g, piece_b, piece_c, piece_dt, piece_log, piece_reset = item
        running, resets_seen, inward, outward, whole_decay = edge_decays(piece_log, piece_reset)
        visible = causal & (resets_seen[:, None] == resets_seen[None, :])
        inner = jnp.where(visible[None], jnp.exp(jnp.minimum(running[:, :, None] - running[:, None, :], 0.0)), 0.0)
        scaled = piece_x * piece_dt.T[:, :, None]
        scores = jnp.dot(piece_c, piece_b.T, precision=highest)
        mixing = inner * scores[None]
        entering = inward.T[:, :, None]
        result = jnp.einsum('hts,shp->thp', mixing, scaled, precision=highest)
        result = result + entering * jnp.einsum('tn,hpn->thp', piece_c, carry_state, precision=highest)
        result = result + skips[None, :, None] * piece_x
        products = jnp.einsum('thp,shp->hts', piece_g, piece_x, precision=highest)
        weight = inner * products * piece_dt[:, None, :]
        grad_x = jnp.einsum('hts,thp->shp', mixing, piece_g, precision=highest) * piece_dt.T[:, :, None]
        grad_x = grad_x + skips[None, :, None] * piece_g
        grad_b = jnp.einsum('hts,tn->sn', weight, piece_c, precision=highest)
        grad_c = jnp.einsum('hts,sn->tn', weight, piece_b, precision=highest)
        grad_c = grad_c + jnp.einsum('hpn,thp->tn', carry_state, piece_g * entering, precision=highest)
        updated = whole_decay[:, None, None] * carry_state + jnp.einsum('shp,sn->hpn', scaled * outward.T[:, :, None], piece_b, precision=highest)
        return updated, (result, grad_x, grad_b, grad_c, inward, outward, whole_decay)

    zeros_state = jnp.zeros((head_count, head_width, bmat.shape[1]), jnp.float32)
    end_state, outs = lax.scan(forward, zeros_state, grouped)
    result, grad_x, grad_b, grad_c, inwards, outwards, wholes = outs

    def backward(carry_grad, item):
        piece_x, piece_g, piece_b, piece_c, piece_dt, inward, outward, whole_decay = item
        factor = (piece_dt * outward).T[:, :, None]
        extra_x = factor * jnp.einsum('hpn,sn->shp', carry_grad, piece_b, precision=highest)
        extra_b = jnp.einsum('hpn,shp->sn', carry_grad, piece_x * factor, precision=highest)
        earlier_grad = whole_decay[:, None, None] * carry_grad + jnp.einsum('thp,tn->hpn', piece_g * inward.T[:, :, None], piece_c, precision=highest)
        return earlier_grad, (extra_x, extra_b)

    start_grad, (extra_x, extra_b) = lax.scan(backward, zeros_state, (grouped[0], grouped[1], grouped[2], grouped[3], grouped[4], inwards, outwards, wholes), reverse=True)
    result = result.reshape(length, head_count, head_width)
    grad_x = (grad_x + extra_x).reshape(length, head_count, head_width)
    grad_b = (grad_b + extra_b).reshape(length, -1)
    grad_c = grad_c.reshape(length, -1)
    return result, grad_x, grad_b, grad_c, end_state, start_grad


def reference(values, input_map, output_map, step_sizes, decay_rates, skip_gains, doc_lengths, out_grad):
    starts = (jnp.cumsum(doc_lengths) - doc_lengths).astype(jnp.int32)
    restart = jnp.zeros((TOKENS,), jnp.float32).at[starts].set(1.0)
    shaped_x = values.reshape(TOKENS, HEADS, HEAD_SIZE)
    shaped_g = out_grad.reshape(TOKENS, HEADS, HEAD_SIZE)
    result, grad_x, grad_b, grad_c, end_state, start_grad = group_pass(shaped_x, input_map, output_map, step_sizes, decay_rates, skip_gains, restart, shaped_g)
    return (result.reshape(TOKENS, -1).astype(jnp.bfloat16), grad_x.reshape(TOKENS, -1).astype(jnp.bfloat16), grad_b, grad_c)
```

```python
import jax
import jax.numpy as jnp
from jax import lax
from jax.experimental import pallas as pl
from jax.experimental.pallas import tpu as pltpu
from jax.sharding import PartitionSpec as P

HEAD_SIZE = 64
STATE = 128
f32 = jnp.float32
bf16 = jnp.bfloat16

NN = (((1,), (0,)), ((), ()))
NT = (((1,), (1,)), ((), ()))


def halves(a):
    high = a.astype(bf16)
    return high, (a - high.astype(f32)).astype(bf16)


def thirds(a):
    high = a.astype(bf16)
    rest = a - high.astype(f32)
    mid = rest.astype(bf16)
    return high, mid, (rest - mid.astype(f32)).astype(bf16)


def dot(a, b, dims):
    return lax.dot_general(a, b, dims, preferred_element_type=f32)


def dot3(a, b, dims):
    return dot(a[0], b[0], dims) + (dot(a[0], b[1], dims) + dot(a[1], b[0], dims))


def spread(cols, heads, width):
    row = lax.broadcasted_iota(jnp.int32, (3 * heads, width), 0)
    lane = lax.broadcasted_iota(jnp.int32, (3 * heads, width), 1)
    first = (row - jnp.where(row >= heads, heads, 0) - jnp.where(row >= 2 * heads, heads, 0)) * HEAD_SIZE
    pick = ((lane >= first) & (lane < first + HEAD_SIZE)).astype(f32).astype(bf16)
    parts = jnp.concatenate([p.astype(f32) for p in thirds(cols)], axis=1).astype(bf16)
    return dot(parts, pick, NN)


def segments(docs, first, length):
    count = docs.shape[1]
    up = lax.broadcasted_iota(jnp.int32, (count, count), 0)
    across = lax.broadcasted_iota(jnp.int32, (count, count), 1)
    start_col = jnp.sum(jnp.where(across < up, docs, 0.0), axis=1, keepdims=True)
    docs_col = jnp.sum(jnp.where(across == up, docs, 0.0), axis=1, keepdims=True)
    start_row = jnp.sum(jnp.where(up < across, docs_col, 0.0), axis=0, keepdims=True)
    at_col = (lax.broadcasted_iota(jnp.int32, (length, 1), 0) + first).astype(f32)
    at_row = (lax.broadcasted_iota(jnp.int32, (1, length), 1) + first).astype(f32)
    seg_col = jnp.sum(jnp.where(start_row <= at_col, 1.0, 0.0), axis=1, keepdims=True)
    seg_row = jnp.sum(jnp.where(start_col <= at_row, 1.0, 0.0), axis=0, keepdims=True)
    before = jnp.sum(jnp.where(start_row < first.astype(f32), 1.0, 0.0), axis=1, keepdims=True)
    return seg_col, seg_row, before


def head_row(ref, heads, width):
    lane = lax.broadcasted_iota(jnp.int32, (1, width), 1)
    out = jnp.zeros((1, width), f32)
    for h in range(heads):
        out = jnp.where((lane >= h * HEAD_SIZE) & (lane < (h + 1) * HEAD_SIZE), ref[h], out)
    return out


def edge_kernel(place, rates, docs, dt, x, g, b, c, send, keep, xh, xl, gh, gl, facts, segs, segr, last):
    length, width = x.shape
    heads = dt.shape[0]
    core = place[0] % 2
    first = place[0] * length
    seg_col, seg_row, before = segments(docs[...].astype(f32), first, length)
    seg_last = seg_col[length - 1 :, :]
    entry = (seg_col == before).astype(f32)
    final = (seg_col == seg_last).astype(f32)
    through = (seg_last == before).astype(f32)

    rate_col = jnp.zeros((heads, 1), f32)
    which = lax.broadcasted_iota(jnp.int32, (heads, 1), 0)
    for h in range(heads):
        rate_col = jnp.where(which == h, rates[h], rate_col)
    steps = dt[...]
    logs = -rate_col * steps
    t_at = lax.broadcasted_iota(jnp.int32, (length, length), 0)
    s_at = lax.broadcasted_iota(jnp.int32, (length, length), 1)
    lower = (s_at <= t_at).astype(f32).astype(bf16)
    eye = (s_at == t_at).astype(f32).astype(bf16)
    run = sum(dot(lower, p, NT) for p in thirds(logs))
    steps_t = sum(dot(eye, p, NT) for p in thirds(steps))
    grow = jnp.exp(run)
    shrink = jnp.exp(-run) * steps_t
    facts[...] = jnp.concatenate([grow, shrink], axis=1)
    col = lax.broadcasted_iota(jnp.int32, (length, 8), 1)
    segs[...] = jnp.where(col == 0, seg_col, jnp.where(col == 1, entry, final))
    segr[...] = jnp.broadcast_to(seg_row, (8, length))

    grow_x = spread(grow, heads, width)
    shrink_x = spread(shrink, heads, width)
    total = grow_x[length - 1 :, :]
    x_parts = halves(x[...] * shrink_x)
    g_parts = halves(g[...] * grow_x)
    xh[...], xl[...] = x_parts
    gh[...], gl[...] = g_parts
    b_parts = halves((b[...] * final).T)
    c_parts = halves((c[...] * entry).T)
    end = dot3(b_parts, x_parts, NN) * total
    start = dot3(c_parts, g_parts, NN)
    last[...] = jnp.broadcast_to(total, (8, width))
    whole = jnp.broadcast_to(total * through, (8, width))
    is_zero = core == 0
    send[:STATE, :] = jnp.where(is_zero, start, end)
    keep[:STATE, :] = jnp.where(is_zero, end, start)
    send[STATE:, :] = whole
    keep[STATE:, :] = whole


def local_kernel(skips, facts, segs, segr, x, g, xh, xl, gh, gl, b, c, y0, z0, grads):
    length, width = x.shape
    heads = facts.shape[1] // 2
    b_parts = halves(b[...])
    c_parts = halves(c[...])
    t_at = lax.broadcasted_iota(jnp.int32, (length, length), 0)
    s_at = lax.broadcasted_iota(jnp.int32, (length, length), 1)
    same = segs[:, :1] == segr[:1, :]
    mask = jnp.where(same & (s_at <= t_at), 1.0, 0.0)
    mask_t = jnp.where(same & (t_at <= s_at), 1.0, 0.0)
    x_parts = (xh[...], xl[...])
    g_parts = (gh[...], gl[...])
    mix = halves(dot3(c_parts, b_parts, NT) * mask)
    mix_t = halves(dot3(b_parts, c_parts, NT) * mask_t)
    skip = head_row(skips, heads, width)
    y0[...] = dot3(mix, x_parts, NN) * spread(facts[:, :heads], heads, width) + skip * x[...]
    z0[...] = dot3(mix_t, g_parts, NN) * spread(facts[:, heads:], heads, width) + skip * g[...]
    weight = dot3(g_parts, x_parts, NT) * mask
    grads[:length, :] = dot3(halves(weight.T), c_parts, NN)
    grads[length:, :] = dot3(halves(weight), b_parts, NN)


def grad_kernel(place, mine, other, last, segs, xh, xl, gh, gl, grads, total):
    length, width = xh.shape
    is_zero = place[0] % 2 == 0
    mine_, other_ = mine[...], other[...]
    into = jnp.where(is_zero, mine_, other_)
    after = jnp.where(is_zero, other_, mine_) * last[:1, :]
    grad_b = dot3((xh[...], xl[...]), halves(after), NT) * segs[:, 2:3]
    grad_c = dot3((gh[...], gl[...]), halves(into), NT) * segs[:, 1:2]
    total[:length, :] = grads[:length, :] + grad_b
    total[length:, :] = grads[length:, :] + grad_c


def out_kernel(place, mine, other, last, facts, segs, b, c, y0, z0, y, z):
    length, width = y0.shape
    heads = facts.shape[1] // 2
    is_zero = place[0] % 2 == 0
    mine_, other_ = mine[...], other[...]
    into = halves(jnp.where(is_zero, mine_, other_))
    after = halves(jnp.where(is_zero, other_, mine_) * last[:1, :])
    c_parts = halves(c[...] * segs[:, 1:2])
    b_parts = halves(b[...] * segs[:, 2:3])
    y[...] = (y0[...] + dot3(c_parts, into, NN) * spread(facts[:, :heads], heads, width)).astype(bf16)
    z[...] = (z0[...] + dot3(b_parts, after, NN) * spread(facts[:, heads:], heads, width)).astype(bf16)


def call(kernel, name, outs, smem, *args):
    specs = [pl.BlockSpec(memory_space=pltpu.SMEM if i in smem else pltpu.VMEM) for i in range(len(args))]
    return pl.pallas_call(
        kernel,
        name=name,
        out_shape=[jax.ShapeDtypeStruct(s, d) for s, d in outs],
        in_specs=specs,
        out_specs=[pl.BlockSpec(memory_space=pltpu.VMEM) for _ in outs],
    )(*args)


def build(seq, head):
    def route(a, target):
        pairs = []
        for s in range(seq):
            for h in range(head):
                s2, h2 = target(s, h)
                if 0 <= s2 < seq:
                    pairs.append((s * head + h, s2 * head + h2))
        return lax.ppermute(a, ("seq", "head"), pairs)

    def partner(a):
        return route(a, lambda s, h: (s ^ 1, h))

    def chips(a, hops):
        return route(a, lambda s, h: (s + 2 * hops if s % 2 == 0 else s - 2 * hops, h))

    def head_sum(a):
        a = a + route(a, lambda s, h: (s, h ^ 1 if s % 2 == 0 else h ^ 3))
        return a + route(a, lambda s, h: (s, h ^ 3 if s % 2 == 0 else h ^ 1))

    def body(x, b, c, dt, rates, skips, docs, g):
        length, width = x.shape
        heads = dt.shape[0]
        place = lax.axis_index("seq").astype(jnp.int32).reshape(1)
        state = (STATE + 8, width)
        wide = (length, width)
        send, keep, xh, xl, gh, gl, facts, segs, segr, last = call(
            edge_kernel, "edges",
            [(state, f32), (state, f32), (wide, bf16), (wide, bf16), (wide, bf16), (wide, bf16),
             ((length, 2 * heads), f32), ((length, 8), f32), ((8, length), f32), ((8, width), f32)],
            (0, 1), place, rates, docs.reshape(1, -1), dt, x, g, b, c)
        got = partner(send)
        row = lax.broadcasted_iota(jnp.int32, state, 0)
        chip = jnp.where(row < STATE, got, 0.0) + got[STATE : STATE + 1] * keep
        near = chips(chip, 1)
        far = chips(chip, 2)
        y0, z0, grads = call(
            local_kernel, "local", [(wide, f32), (wide, f32), ((2 * length, STATE), f32)],
            (0,), skips, facts, segs, segr, x, g, xh, xl, gh, gl, b, c)
        mine = near[:STATE] + near[STATE : STATE + 1] * far[:STATE]
        other = partner(keep[:STATE] + keep[STATE : STATE + 1] * mine)
        (part,) = call(
            grad_kernel, "grads", [((2 * length, STATE), f32)],
            (0,), place, mine, other, last, segs, xh, xl, gh, gl, grads)
        y, z = call(
            out_kernel, "outs", [(wide, bf16), (wide, bf16)],
            (0,), place, mine, other, last, facts, segs, b, c, y0, z0)
        summed = head_sum(part)
        return y, z, summed[:length], summed[length:]

    return body


def solution(mesh):
    wide = P("seq", "head")
    row = P("seq", None)
    return jax.shard_map(
        build(mesh.shape["seq"], mesh.shape["head"]),
        mesh=mesh,
        in_specs=(wide, row, row, P("head", "seq"), P("head"), P("head"), P(), wide),
        out_specs=(wide, wide, row, row),
        check_vma=False,
    )
```

```python
import jax
import jax.numpy as jnp
from jax import lax
from jax.experimental import pallas as pl
from jax.experimental.pallas import tpu as pltpu
from jax.sharding import PartitionSpec as P

HEAD_SIZE = 64
STATE = 128
f32 = jnp.float32
bf16 = jnp.bfloat16

NN = (((1,), (0,)), ((), ()))
NT = (((1,), (1,)), ((), ()))


def halves(a):
    high = a.astype(bf16)
    return high, (a - high.astype(f32)).astype(bf16)


def thirds(a):
    high = a.astype(bf16)
    rest = a - high.astype(f32)
    mid = rest.astype(bf16)
    return high, mid, (rest - mid.astype(f32)).astype(bf16)


def dot(a, b, dims):
    return lax.dot_general(a, b, dims, preferred_element_type=f32)


def dot3(a, b, dims):
    return dot(a[0], b[0], dims) + (dot(a[0], b[1], dims) + dot(a[1], b[0], dims))


def spread(cols, heads, width):
    row = lax.broadcasted_iota(jnp.int32, (3 * heads, width), 0)
    lane = lax.broadcasted_iota(jnp.int32, (3 * heads, width), 1)
    first = (row - jnp.where(row >= heads, heads, 0) - jnp.where(row >= 2 * heads, heads, 0)) * HEAD_SIZE
    pick = ((lane >= first) & (lane < first + HEAD_SIZE)).astype(f32).astype(bf16)
    parts = jnp.concatenate([p.astype(f32) for p in thirds(cols)], axis=1).astype(bf16)
    return dot(parts, pick, NN)


def segments(docs, first, length):
    count = docs.shape[1]
    up = lax.broadcasted_iota(jnp.int32, (count, count), 0)
    across = lax.broadcasted_iota(jnp.int32, (count, count), 1)
    start_col = jnp.sum(jnp.where(across < up, docs, 0.0), axis=1, keepdims=True)
    docs_col = jnp.sum(jnp.where(across == up, docs, 0.0), axis=1, keepdims=True)
    start_row = jnp.sum(jnp.where(up < across, docs_col, 0.0), axis=0, keepdims=True)
    at_col = (lax.broadcasted_iota(jnp.int32, (length, 1), 0) + first).astype(f32)
    at_row = (lax.broadcasted_iota(jnp.int32, (1, length), 1) + first).astype(f32)
    seg_col = jnp.sum(jnp.where(start_row <= at_col, 1.0, 0.0), axis=1, keepdims=True)
    seg_row = jnp.sum(jnp.where(start_col <= at_row, 1.0, 0.0), axis=0, keepdims=True)
    before = jnp.sum(jnp.where(start_row < first.astype(f32), 1.0, 0.0), axis=1, keepdims=True)
    return seg_col, seg_row, before


def head_row(ref, heads, width):
    lane = lax.broadcasted_iota(jnp.int32, (1, width), 1)
    out = jnp.zeros((1, width), f32)
    for h in range(heads):
        out = jnp.where((lane >= h * HEAD_SIZE) & (lane < (h + 1) * HEAD_SIZE), ref[h], out)
    return out


def edge_kernel(place, rates, docs, dt, x, g, b, c, send, keep, xh, xl, gh, gl, facts, segs, segr, last):
    length, width = x.shape
    heads = dt.shape[0]
    core = place[0] % 2
    first = place[0] * length
    seg_col, seg_row, before = segments(docs[...].astype(f32), first, length)
    seg_last = seg_col[length - 1 :, :]
    entry = (seg_col == before).astype(f32)
    final = (seg_col == seg_last).astype(f32)
    through = (seg_last == before).astype(f32)

    rate_col = jnp.zeros((heads, 1), f32)
    which = lax.broadcasted_iota(jnp.int32, (heads, 1), 0)
    for h in range(heads):
        rate_col = jnp.where(which == h, rates[h], rate_col)
    steps = dt[...]
    logs = -rate_col * steps
    t_at = lax.broadcasted_iota(jnp.int32, (length, length), 0)
    s_at = lax.broadcasted_iota(jnp.int32, (length, length), 1)
    lower = (s_at <= t_at).astype(f32).astype(bf16)
    eye = (s_at == t_at).astype(f32).astype(bf16)
    run = sum(dot(lower, p, NT) for p in thirds(logs))
    steps_t = sum(dot(eye, p, NT) for p in thirds(steps))
    grow = jnp.exp(run)
    shrink = jnp.exp(-run) * steps_t
    facts[...] = jnp.concatenate([grow, shrink], axis=1)
    col = lax.broadcasted_iota(jnp.int32, (length, 8), 1)
    segs[...] = jnp.where(col == 0, seg_col, jnp.where(col == 1, entry, final))
    segr[...] = jnp.broadcast_to(seg_row, (8, length))

    grow_x = spread(grow, heads, width)
    shrink_x = spread(shrink, heads, width)
    total = grow_x[length - 1 :, :]
    x_parts = halves(x[...] * shrink_x)
    g_parts = halves(g[...] * grow_x)
    xh[...], xl[...] = x_parts
    gh[...], gl[...] = g_parts
    b_parts = halves((b[...] * final).T)
    c_parts = halves((c[...] * entry).T)
    end = dot3(b_parts, x_parts, NN) * total
    start = dot3(c_parts, g_parts, NN)
    last[...] = jnp.broadcast_to(total, (8, width))
    whole = jnp.broadcast_to(total * through, (8, width))
    is_zero = core == 0
    send[:STATE, :] = jnp.where(is_zero, start, end)
    keep[:STATE, :] = jnp.where(is_zero, end, start)
    send[STATE:, :] = whole
    keep[STATE:, :] = whole


def local_kernel(skips, facts, segs, segr, x, g, xh, xl, gh, gl, b, c, y0, z0, grads):
    length, width = x.shape
    heads = facts.shape[1] // 2
    b_parts = halves(b[...])
    c_parts = halves(c[...])
    t_at = lax.broadcasted_iota(jnp.int32, (length, length), 0)
    s_at = lax.broadcasted_iota(jnp.int32, (length, length), 1)
    same = segs[:, :1] == segr[:1, :]
    mask = jnp.where(same & (s_at <= t_at), 1.0, 0.0)
    mask_t = jnp.where(same & (t_at <= s_at), 1.0, 0.0)
    x_parts = (xh[...], xl[...])
    g_parts = (gh[...], gl[...])
    mix = halves(dot3(c_parts, b_parts, NT) * mask)
    mix_t = halves(dot3(b_parts, c_parts, NT) * mask_t)
    skip = head_row(skips, heads, width)
    y0[...] = dot3(mix, x_parts, NN) * spread(facts[:, :heads], heads, width) + skip * x[...]
    z0[...] = dot3(mix_t, g_parts, NN) * spread(facts[:, heads:], heads, width) + skip * g[...]
    weight = dot3(g_parts, x_parts, NT) * mask
    grads[:length, :] = dot3(halves(weight.T), c_parts, NN)
    grads[length:, :] = dot3(halves(weight), b_parts, NN)


def grad_kernel(place, mine, other, last, segs, xh, xl, gh, gl, grads, total):
    length, width = xh.shape
    is_zero = place[0] % 2 == 0
    mine_, other_ = mine[...], other[...]
    into = jnp.where(is_zero, mine_, other_)
    after = jnp.where(is_zero, other_, mine_) * last[:1, :]
    grad_b = dot3((xh[...], xl[...]), halves(after), NT) * segs[:, 2:3]
    grad_c = dot3((gh[...], gl[...]), halves(into), NT) * segs[:, 1:2]
    total[:length, :] = grads[:length, :] + grad_b
    total[length:, :] = grads[length:, :] + grad_c


def out_kernel(place, mine, other, last, facts, segs, b, c, y0, z0, y, z):
    length, width = y0.shape
    heads = facts.shape[1] // 2
    is_zero = place[0] % 2 == 0
    mine_, other_ = mine[...], other[...]
    into = halves(jnp.where(is_zero, mine_, other_))
    after = halves(jnp.where(is_zero, other_, mine_) * last[:1, :])
    c_parts = halves(c[...] * segs[:, 1:2])
    b_parts = halves(b[...] * segs[:, 2:3])
    y[...] = (y0[...] + dot3(c_parts, into, NN) * spread(facts[:, :heads], heads, width)).astype(bf16)
    z[...] = (z0[...] + dot3(b_parts, after, NN) * spread(facts[:, heads:], heads, width)).astype(bf16)


def call(kernel, name, outs, smem, *args):
    specs = [pl.BlockSpec(memory_space=pltpu.SMEM if i in smem else pltpu.VMEM) for i in range(len(args))]
    return pl.pallas_call(
        kernel,
        name=name,
        out_shape=[jax.ShapeDtypeStruct(s, d) for s, d in outs],
        in_specs=specs,
        out_specs=[pl.BlockSpec(memory_space=pltpu.VMEM) for _ in outs],
    )(*args)


def build(seq, head):
    def route(a, target):
        pairs = []
        for s in range(seq):
            for h in range(head):
                s2, h2 = target(s, h)
                if 0 <= s2 < seq:
                    pairs.append((s * head + h, s2 * head + h2))
        return lax.ppermute(a, ("seq", "head"), pairs)

    def partner(a):
        return route(a, lambda s, h: (s ^ 1, h))

    def chips(a):
        return route(a, lambda s, h: (s + 2 if s % 2 == 0 else s - 2, h))

    def head_sum(a):
        a = a + route(a, lambda s, h: (s, h ^ 1 if s % 2 == 0 else h ^ 3))
        return a + route(a, lambda s, h: (s, h ^ 3 if s % 2 == 0 else h ^ 1))

    def body(x, b, c, dt, rates, skips, docs, g):
        length, width = x.shape
        heads = dt.shape[0]
        place = lax.axis_index("seq").astype(jnp.int32).reshape(1)
        state = (STATE + 8, width)
        wide = (length, width)
        send, keep, xh, xl, gh, gl, facts, segs, segr, last = call(
            edge_kernel, "edges",
            [(state, f32), (state, f32), (wide, bf16), (wide, bf16), (wide, bf16), (wide, bf16),
             ((length, 2 * heads), f32), ((length, 8), f32), ((8, length), f32), ((8, width), f32)],
            (0, 1), place, rates, docs.reshape(1, -1), dt, x, g, b, c)
        got = partner(send)
        state_out = got[:STATE] + got[STATE : STATE + 1] * keep[:STATE]
        fade = got[STATE : STATE + 1] * keep[STATE : STATE + 1]
        near = chips(state_out)
        y0, z0, grads = call(
            local_kernel, "local", [(wide, f32), (wide, f32), ((2 * length, STATE), f32)],
            (0,), skips, facts, segs, segr, x, g, xh, xl, gh, gl, b, c)
        near, grads = lax.optimization_barrier((near, grads))
        mine = chips(state_out + fade * near)
        other = partner(keep[:STATE] + keep[STATE : STATE + 1] * mine)
        (part,) = call(
            grad_kernel, "grads", [((2 * length, STATE), f32)],
            (0,), place, mine, other, last, segs, xh, xl, gh, gl, grads)
        y, z = call(
            out_kernel, "outs", [(wide, bf16), (wide, bf16)],
            (0,), place, mine, other, last, facts, segs, b, c, y0, z0)
        summed = head_sum(part)
        return y, z, summed[:length], summed[length:]

    return body


def solution(mesh):
    wide = P("seq", "head")
    row = P("seq", None)
    return jax.shard_map(
        build(mesh.shape["seq"], mesh.shape["head"]),
        mesh=mesh,
        in_specs=(wide, row, row, P("head", "seq"), P("head"), P("head"), P(), wide),
        out_specs=(wide, wide, row, row),
        check_vma=False,
    )
```

```python
from functools import partial

import jax
import jax.numpy as jnp
from jax import lax
from jax.experimental import pallas as pl
from jax.experimental.pallas import tpu as pltpu
from jax.sharding import PartitionSpec as P

HEAD_SIZE = 64
STATE = 128
f32 = jnp.float32
bf16 = jnp.bfloat16

NN = (((1,), (0,)), ((), ()))
NT = (((1,), (1,)), ((), ()))


def halves(a):
    high = a.astype(bf16)
    return high, (a - high.astype(f32)).astype(bf16)


def thirds(a):
    high = a.astype(bf16)
    rest = a - high.astype(f32)
    mid = rest.astype(bf16)
    return high, mid, (rest - mid.astype(f32)).astype(bf16)


def dot(a, b, dims):
    return lax.dot_general(a, b, dims, preferred_element_type=f32)


def dot3(a, b, dims):
    return dot(a[0], b[0], dims) + (dot(a[0], b[1], dims) + dot(a[1], b[0], dims))


def spread(cols, heads, width):
    row = lax.broadcasted_iota(jnp.int32, (3 * heads, width), 0)
    lane = lax.broadcasted_iota(jnp.int32, (3 * heads, width), 1)
    first = (row - jnp.where(row >= heads, heads, 0) - jnp.where(row >= 2 * heads, heads, 0)) * HEAD_SIZE
    pick = ((lane >= first) & (lane < first + HEAD_SIZE)).astype(f32).astype(bf16)
    parts = jnp.concatenate([p.astype(f32) for p in thirds(cols)], axis=1).astype(bf16)
    return dot(parts, pick, NN)


def segments(docs, first, length):
    count = docs.shape[1]
    up = lax.broadcasted_iota(jnp.int32, (count, count), 0)
    across = lax.broadcasted_iota(jnp.int32, (count, count), 1)
    start_col = jnp.sum(jnp.where(across < up, docs, 0.0), axis=1, keepdims=True)
    docs_col = jnp.sum(jnp.where(across == up, docs, 0.0), axis=1, keepdims=True)
    start_row = jnp.sum(jnp.where(up < across, docs_col, 0.0), axis=0, keepdims=True)
    at_col = (lax.broadcasted_iota(jnp.int32, (length, 1), 0) + first).astype(f32)
    at_row = (lax.broadcasted_iota(jnp.int32, (1, length), 1) + first).astype(f32)
    seg_col = jnp.sum(jnp.where(start_row <= at_col, 1.0, 0.0), axis=1, keepdims=True)
    seg_row = jnp.sum(jnp.where(start_col <= at_row, 1.0, 0.0), axis=0, keepdims=True)
    before = jnp.sum(jnp.where(start_row < first.astype(f32), 1.0, 0.0), axis=1, keepdims=True)
    return seg_col, seg_row, before


def head_row(ref, heads, width):
    lane = lax.broadcasted_iota(jnp.int32, (1, width), 1)
    out = jnp.zeros((1, width), f32)
    for h in range(heads):
        out = jnp.where((lane >= h * HEAD_SIZE) & (lane < (h + 1) * HEAD_SIZE), ref[h], out)
    return out


def edge_kernel(place, rates, docs, dt, x, g, b, c, send, keep, mh, ml, oh, ol, facts, segs, segr, last):
    length, width = x.shape
    heads = dt.shape[0]
    core = place[0] % 2
    first = place[0] * length
    seg_col, seg_row, before = segments(docs[...].astype(f32), first, length)
    seg_last = seg_col[length - 1 :, :]
    entry = (seg_col == before).astype(f32)
    final = (seg_col == seg_last).astype(f32)
    through = (seg_last == before).astype(f32)

    rate_col = jnp.zeros((heads, 1), f32)
    which = lax.broadcasted_iota(jnp.int32, (heads, 1), 0)
    for h in range(heads):
        rate_col = jnp.where(which == h, rates[h], rate_col)
    steps = dt[...]
    logs = -rate_col * steps
    t_at = lax.broadcasted_iota(jnp.int32, (length, length), 0)
    s_at = lax.broadcasted_iota(jnp.int32, (length, length), 1)
    lower = (s_at <= t_at).astype(f32).astype(bf16)
    eye = (s_at == t_at).astype(f32).astype(bf16)
    run = sum(dot(lower, p, NT) for p in thirds(logs))
    steps_t = sum(dot(eye, p, NT) for p in thirds(steps))
    grow = jnp.exp(run)
    shrink = jnp.exp(-run) * steps_t
    facts[...] = jnp.concatenate([grow, shrink], axis=1)
    col = lax.broadcasted_iota(jnp.int32, (length, 8), 1)
    segs[...] = jnp.where(col == 0, seg_col, jnp.where(col == 1, entry, final))
    segr[...] = jnp.broadcast_to(seg_row, (8, length))

    grow_x = spread(grow, heads, width)
    shrink_x = spread(shrink, heads, width)
    total = grow_x[length - 1 :, :]
    x_parts = halves(x[...] * shrink_x)
    g_parts = halves(g[...] * grow_x)
    is_zero = core == 0

    @pl.when(is_zero)
    def _():
        mh[...], ml[...] = g_parts
        oh[...], ol[...] = x_parts

    @pl.when(core == 1)
    def _():
        mh[...], ml[...] = x_parts
        oh[...], ol[...] = g_parts

    b_parts = halves((b[...] * final).T)
    c_parts = halves((c[...] * entry).T)
    end = dot3(b_parts, x_parts, NN) * total
    start = dot3(c_parts, g_parts, NN)
    last[...] = jnp.broadcast_to(total, (8, width))
    whole = jnp.broadcast_to(total * through, (8, width))
    send[:STATE, :] = jnp.where(is_zero, start, end)
    keep[:STATE, :] = jnp.where(is_zero, end, start)
    send[STATE:, :] = whole
    keep[STATE:, :] = whole


def local_kernel(place, skips, facts, segs, segr, x, g, mh, ml, oh, ol, b, c, y0, z0, mine, other):
    length, width = x.shape
    heads = facts.shape[1] // 2
    b_parts = halves(b[...])
    c_parts = halves(c[...])
    t_at = lax.broadcasted_iota(jnp.int32, (length, length), 0)
    s_at = lax.broadcasted_iota(jnp.int32, (length, length), 1)
    same = segs[:, :1] == segr[:1, :]
    mask = jnp.where(same & (s_at <= t_at), 1.0, 0.0)
    mask_t = jnp.where(same & (t_at <= s_at), 1.0, 0.0)
    core = place[0] % 2
    m_parts = (mh[...], ml[...])
    o_parts = (oh[...], ol[...])
    x_parts = [jnp.where(core == 0, o, m) for m, o in zip(m_parts, o_parts)]
    g_parts = [jnp.where(core == 0, m, o) for m, o in zip(m_parts, o_parts)]
    mix = halves(dot3(c_parts, b_parts, NT) * mask)
    mix_t = halves(dot3(b_parts, c_parts, NT) * mask_t)
    skip = head_row(skips, heads, width)
    y0[...] = dot3(mix, x_parts, NN) * spread(facts[:, :heads], heads, width) + skip * x[...]
    z0[...] = dot3(mix_t, g_parts, NN) * spread(facts[:, heads:], heads, width) + skip * g[...]
    weight = dot3(g_parts, x_parts, NT) * mask
    grad_b = dot3(halves(weight.T), c_parts, NN)
    grad_c = dot3(halves(weight), b_parts, NN)
    mine[...] = jnp.where(core == 0, grad_c, grad_b)
    other[...] = jnp.where(core == 0, grad_b, grad_c)


def grad_kernel(core, place, state, last, segs, high, low, local, total):
    is_forward = place[0] % 2 == core
    scale = jnp.where(is_forward, 1.0, last[:1, :])
    tokens = jnp.where(is_forward, segs[:, 1:2], segs[:, 2:3])
    total[...] = local[...] + dot3((high[...], low[...]), halves(state[...] * scale), NT) * tokens


def out_kernel(place, mine, other, last, facts, segs, b, c, y0, z0, y, z):
    length, width = y0.shape
    heads = facts.shape[1] // 2
    is_zero = place[0] % 2 == 0
    mine_, other_ = mine[...], other[...]
    into = halves(jnp.where(is_zero, mine_, other_))
    after = halves(jnp.where(is_zero, other_, mine_) * last[:1, :])
    c_parts = halves(c[...] * segs[:, 1:2])
    b_parts = halves(b[...] * segs[:, 2:3])
    y[...] = (y0[...] + dot3(c_parts, into, NN) * spread(facts[:, :heads], heads, width)).astype(bf16)
    z[...] = (z0[...] + dot3(b_parts, after, NN) * spread(facts[:, heads:], heads, width)).astype(bf16)


def call(kernel, name, outs, smem, *args):
    specs = [pl.BlockSpec(memory_space=pltpu.SMEM if i in smem else pltpu.VMEM) for i in range(len(args))]
    return pl.pallas_call(
        kernel,
        name=name,
        out_shape=[jax.ShapeDtypeStruct(s, d) for s, d in outs],
        in_specs=specs,
        out_specs=[pl.BlockSpec(memory_space=pltpu.VMEM) for _ in outs],
    )(*args)


def build(seq, head):
    def route(a, target):
        pairs = []
        for s in range(seq):
            for h in range(head):
                s2, h2 = target(s, h)
                if 0 <= s2 < seq:
                    pairs.append((s * head + h, s2 * head + h2))
        return lax.ppermute(a, ("seq", "head"), pairs)

    def partner(a):
        return route(a, lambda s, h: (s ^ 1, h))

    def chips(a):
        return route(a, lambda s, h: (s + 2 if s % 2 == 0 else s - 2, h))

    def head_sum(a):
        a = a + route(a, lambda s, h: (s, h ^ 1 if s % 2 == 0 else h ^ 3))
        return a + route(a, lambda s, h: (s, h ^ 3 if s % 2 == 0 else h ^ 1))

    def body(x, b, c, dt, rates, skips, docs, g):
        length, width = x.shape
        heads = dt.shape[0]
        place = lax.axis_index("seq").astype(jnp.int32).reshape(1)
        state = (STATE + 8, width)
        wide = (length, width)
        send, keep, mh, ml, oh, ol, facts, segs, segr, last = call(
            edge_kernel, "edges",
            [(state, f32), (state, f32), (wide, bf16), (wide, bf16), (wide, bf16), (wide, bf16),
             ((length, 2 * heads), f32), ((length, 8), f32), ((8, length), f32), ((8, width), f32)],
            (0, 1), place, rates, docs.reshape(1, -1), dt, x, g, b, c)
        got = partner(send)
        state_out = got[:STATE] + got[STATE : STATE + 1] * keep[:STATE]
        fade = got[STATE : STATE + 1] * keep[STATE : STATE + 1]
        near = chips(state_out)
        thin = ((length, STATE), f32)
        y0, z0, mine0, other0 = call(
            local_kernel, "local", [(wide, f32), (wide, f32), thin, thin],
            (0, 1), place, skips, facts, segs, segr, x, g, mh, ml, oh, ol, b, c)
        near, mine0 = lax.optimization_barrier((near, mine0))
        mine = chips(state_out + fade * near)
        other = partner(keep[:STATE] + keep[STATE : STATE + 1] * mine)
        (first,) = call(partial(grad_kernel, 0), "first", [thin], (0,), place, mine, last, segs, mh, ml, mine0)
        (second,) = call(partial(grad_kernel, 1), "second", [thin], (0,), place, other, last, segs, oh, ol, other0)
        y, z = call(
            out_kernel, "outs", [(wide, bf16), (wide, bf16)],
            (0,), place, mine, other, last, facts, segs, b, c, y0, z0)
        first = head_sum(first)
        second = head_sum(second)
        zero = (place[0] & 1) == 0
        return y, z, jnp.where(zero, second, first), jnp.where(zero, first, second)

    return body


def solution(mesh):
    wide = P("seq", "head")
    row = P("seq", None)
    return jax.shard_map(
        build(mesh.shape["seq"], mesh.shape["head"]),
        mesh=mesh,
        in_specs=(wide, row, row, P("head", "seq"), P("head"), P("head"), P(), wide),
        out_specs=(wide, wide, row, row),
        check_vma=False,
    )
```

```python
from functools import partial

import jax
import jax.numpy as jnp
from jax import lax
from jax.experimental import pallas as pl
from jax.experimental.pallas import tpu as pltpu
from jax.sharding import PartitionSpec as P

HEAD_SIZE = 64
STATE = 128
f32 = jnp.float32
bf16 = jnp.bfloat16

NN = (((1,), (0,)), ((), ()))
NT = (((1,), (1,)), ((), ()))


def halves(a):
    high = a.astype(bf16)
    return high, (a - high.astype(f32)).astype(bf16)


def thirds(a):
    high = a.astype(bf16)
    rest = a - high.astype(f32)
    mid = rest.astype(bf16)
    return high, mid, (rest - mid.astype(f32)).astype(bf16)


def dot(a, b, dims):
    return lax.dot_general(a, b, dims, preferred_element_type=f32)


def dot3(a, b, dims):
    return dot(a[0], b[0], dims) + (dot(a[0], b[1], dims) + dot(a[1], b[0], dims))


def spread(cols, heads, width):
    row = lax.broadcasted_iota(jnp.int32, (3 * heads, width), 0)
    lane = lax.broadcasted_iota(jnp.int32, (3 * heads, width), 1)
    first = (row - jnp.where(row >= heads, heads, 0) - jnp.where(row >= 2 * heads, heads, 0)) * HEAD_SIZE
    pick = ((lane >= first) & (lane < first + HEAD_SIZE)).astype(f32).astype(bf16)
    parts = jnp.concatenate([p.astype(f32) for p in thirds(cols)], axis=1).astype(bf16)
    return dot(parts, pick, NN)


def segments(docs, first, length):
    count = docs.shape[1]
    up = lax.broadcasted_iota(jnp.int32, (count, count), 0)
    across = lax.broadcasted_iota(jnp.int32, (count, count), 1)
    start_col = jnp.sum(jnp.where(across < up, docs, 0.0), axis=1, keepdims=True)
    docs_col = jnp.sum(jnp.where(across == up, docs, 0.0), axis=1, keepdims=True)
    start_row = jnp.sum(jnp.where(up < across, docs_col, 0.0), axis=0, keepdims=True)
    at_col = (lax.broadcasted_iota(jnp.int32, (length, 1), 0) + first).astype(f32)
    at_row = (lax.broadcasted_iota(jnp.int32, (1, length), 1) + first).astype(f32)
    seg_col = jnp.sum(jnp.where(start_row <= at_col, 1.0, 0.0), axis=1, keepdims=True)
    seg_row = jnp.sum(jnp.where(start_col <= at_row, 1.0, 0.0), axis=0, keepdims=True)
    before = jnp.sum(jnp.where(start_row < first.astype(f32), 1.0, 0.0), axis=1, keepdims=True)
    return seg_col, seg_row, before


def head_row(ref, heads, width):
    lane = lax.broadcasted_iota(jnp.int32, (1, width), 1)
    out = jnp.zeros((1, width), f32)
    for h in range(heads):
        out = jnp.where((lane >= h * HEAD_SIZE) & (lane < (h + 1) * HEAD_SIZE), ref[h], out)
    return out


def edge_kernel(place, rates, docs, dt, x, g, b, c, send, keep, mh, ml, oh, ol, facts, segs, segr, last):
    length, width = x.shape
    heads = dt.shape[0]
    core = place[0] % 2
    first = place[0] * length
    seg_col, seg_row, before = segments(docs[...].astype(f32), first, length)
    seg_last = seg_col[length - 1 :, :]
    entry = (seg_col == before).astype(f32)
    final = (seg_col == seg_last).astype(f32)
    through = (seg_last == before).astype(f32)

    rate_col = jnp.zeros((heads, 1), f32)
    which = lax.broadcasted_iota(jnp.int32, (heads, 1), 0)
    for h in range(heads):
        rate_col = jnp.where(which == h, rates[h], rate_col)
    steps = dt[...]
    logs = -rate_col * steps
    t_at = lax.broadcasted_iota(jnp.int32, (length, length), 0)
    s_at = lax.broadcasted_iota(jnp.int32, (length, length), 1)
    lower = (s_at <= t_at).astype(f32).astype(bf16)
    eye = (s_at == t_at).astype(f32).astype(bf16)
    run = sum(dot(lower, p, NT) for p in thirds(logs))
    steps_t = sum(dot(eye, p, NT) for p in thirds(steps))
    grow = jnp.exp(run)
    shrink = jnp.exp(-run) * steps_t
    facts[...] = jnp.concatenate([grow, shrink], axis=1)
    col = lax.broadcasted_iota(jnp.int32, (length, 8), 1)
    segs[...] = jnp.where(col == 0, seg_col, jnp.where(col == 1, entry, final))
    segr[...] = jnp.broadcast_to(seg_row, (8, length))

    grow_x = spread(grow, heads, width)
    shrink_x = spread(shrink, heads, width)
    total = grow_x[length - 1 :, :]
    x_parts = halves(x[...] * shrink_x)
    g_parts = halves(g[...] * grow_x)
    is_zero = core == 0

    @pl.when(is_zero)
    def _():
        mh[...], ml[...] = g_parts
        oh[...], ol[...] = x_parts

    @pl.when(core == 1)
    def _():
        mh[...], ml[...] = x_parts
        oh[...], ol[...] = g_parts

    b_parts = halves((b[...] * final).T)
    c_parts = halves((c[...] * entry).T)
    end = dot3(b_parts, x_parts, NN) * total
    start = dot3(c_parts, g_parts, NN)
    last[...] = jnp.broadcast_to(total, (8, width))
    whole = jnp.broadcast_to(total * through, (8, width))
    send[:STATE, :] = jnp.where(is_zero, start, end)
    keep[:STATE, :] = jnp.where(is_zero, end, start)
    send[STATE:, :] = whole
    keep[STATE:, :] = whole


def local_kernel(place, skips, facts, segs, segr, x, g, mh, ml, oh, ol, b, c, y0, z0, mine, other):
    length, width = x.shape
    heads = facts.shape[1] // 2
    b_parts = halves(b[...])
    c_parts = halves(c[...])
    t_at = lax.broadcasted_iota(jnp.int32, (length, length), 0)
    s_at = lax.broadcasted_iota(jnp.int32, (length, length), 1)
    same = segs[:, :1] == segr[:1, :]
    mask = jnp.where(same & (s_at <= t_at), 1.0, 0.0)
    mask_t = jnp.where(same & (t_at <= s_at), 1.0, 0.0)
    core = place[0] % 2
    m_parts = (mh[...], ml[...])
    o_parts = (oh[...], ol[...])
    x_parts = [jnp.where(core == 0, o, m) for m, o in zip(m_parts, o_parts)]
    g_parts = [jnp.where(core == 0, m, o) for m, o in zip(m_parts, o_parts)]
    mix = halves(dot3(c_parts, b_parts, NT) * mask)
    mix_t = halves(dot3(b_parts, c_parts, NT) * mask_t)
    skip = head_row(skips, heads, width)
    y0[...] = dot3(mix, x_parts, NN) * spread(facts[:, :heads], heads, width) + skip * x[...]
    z0[...] = dot3(mix_t, g_parts, NN) * spread(facts[:, heads:], heads, width) + skip * g[...]
    weight = dot3(g_parts, x_parts, NT) * mask
    grad_b = dot3(halves(weight.T), c_parts, NN)
    grad_c = dot3(halves(weight), b_parts, NN)
    mine[...] = jnp.where(core == 0, grad_c, grad_b)
    other[...] = jnp.where(core == 0, grad_b, grad_c)


def grad_kernel(core, place, state, last, segs, high, low, local, total):
    is_forward = place[0] % 2 == core
    scale = jnp.where(is_forward, 1.0, last[:1, :])
    tokens = jnp.where(is_forward, segs[:, 1:2], segs[:, 2:3])
    total[...] = local[...] + dot3((high[...], low[...]), halves(state[...] * scale), NT) * tokens


def out_kernel(place, mine, other, last, facts, segs, b, c, y0, z0, y, z):
    length, width = y0.shape
    heads = facts.shape[1] // 2
    is_zero = place[0] % 2 == 0
    mine_, other_ = mine[...], other[...]
    into = halves(jnp.where(is_zero, mine_, other_))
    after = halves(jnp.where(is_zero, other_, mine_) * last[:1, :])
    c_parts = halves(c[...] * segs[:, 1:2])
    b_parts = halves(b[...] * segs[:, 2:3])
    y[...] = (y0[...] + dot3(c_parts, into, NN) * spread(facts[:, :heads], heads, width)).astype(bf16)
    z[...] = (z0[...] + dot3(b_parts, after, NN) * spread(facts[:, heads:], heads, width)).astype(bf16)


def call(kernel, name, outs, smem, *args):
    specs = [pl.BlockSpec(memory_space=pltpu.SMEM if i in smem else pltpu.VMEM) for i in range(len(args))]
    return pl.pallas_call(
        kernel,
        name=name,
        out_shape=[jax.ShapeDtypeStruct(s, d) for s, d in outs],
        in_specs=specs,
        out_specs=[pl.BlockSpec(memory_space=pltpu.VMEM) for _ in outs],
    )(*args)


def build(seq, head):
    def route(a, target):
        pairs = []
        for s in range(seq):
            for h in range(head):
                s2, h2 = target(s, h)
                if 0 <= s2 < seq:
                    pairs.append((s * head + h, s2 * head + h2))
        return lax.ppermute(a, ("seq", "head"), pairs)

    def partner(a):
        return route(a, lambda s, h: (s ^ 1, h))

    def chips(a, hops):
        return route(a, lambda s, h: (s + 2 * hops if s % 2 == 0 else s - 2 * hops, h))

    def head_sum(a):
        a = a + route(a, lambda s, h: (s, h ^ 1 if s % 2 == 0 else h ^ 3))
        return a + route(a, lambda s, h: (s, h ^ 3 if s % 2 == 0 else h ^ 1))

    def body(x, b, c, dt, rates, skips, docs, g):
        length, width = x.shape
        heads = dt.shape[0]
        place = lax.axis_index("seq").astype(jnp.int32).reshape(1)
        state = (STATE + 8, width)
        wide = (length, width)
        send, keep, mh, ml, oh, ol, facts, segs, segr, last = call(
            edge_kernel, "edges",
            [(state, f32), (state, f32), (wide, bf16), (wide, bf16), (wide, bf16), (wide, bf16),
             ((length, 2 * heads), f32), ((length, 8), f32), ((8, length), f32), ((8, width), f32)],
            (0, 1), place, rates, docs.reshape(1, -1), dt, x, g, b, c)
        got = partner(send)
        row = lax.broadcasted_iota(jnp.int32, state, 0)
        chip = jnp.where(row < STATE, got, 0.0) + got[STATE : STATE + 1] * keep
        far = chips(chip, 2)
        near = chips(chip, 1)
        thin = ((length, STATE), f32)
        y0, z0, mine0, other0 = call(
            local_kernel, "local", [(wide, f32), (wide, f32), thin, thin],
            (0, 1), place, skips, facts, segs, segr, x, g, mh, ml, oh, ol, b, c)
        near, far, mine0 = lax.optimization_barrier((near, far, mine0))
        mine = near[:STATE] + near[STATE : STATE + 1] * far[:STATE]
        other = partner(keep[:STATE] + keep[STATE : STATE + 1] * mine)
        (first,) = call(partial(grad_kernel, 0), "first", [thin], (0,), place, mine, last, segs, mh, ml, mine0)
        (second,) = call(partial(grad_kernel, 1), "second", [thin], (0,), place, other, last, segs, oh, ol, other0)
        y, z = call(
            out_kernel, "outs", [(wide, bf16), (wide, bf16)],
            (0,), place, mine, other, last, facts, segs, b, c, y0, z0)
        first = head_sum(first)
        second = head_sum(second)
        zero = (place[0] & 1) == 0
        return y, z, jnp.where(zero, second, first), jnp.where(zero, first, second)

    return body


def solution(mesh):
    wide = P("seq", "head")
    row = P("seq", None)
    return jax.shard_map(
        build(mesh.shape["seq"], mesh.shape["head"]),
        mesh=mesh,
        in_specs=(wide, row, row, P("head", "seq"), P("head"), P("head"), P(), wide),
        out_specs=(wide, wide, row, row),
        check_vma=False,
    )
```

```python
from functools import partial

import jax
import jax.numpy as jnp
from jax import lax
from jax.experimental import pallas as pl
from jax.experimental.pallas import tpu as pltpu
from jax.sharding import PartitionSpec as P

HEAD_SIZE = 64
STATE = 128
f32 = jnp.float32
bf16 = jnp.bfloat16

NN = (((1,), (0,)), ((), ()))
NT = (((1,), (1,)), ((), ()))


def halves(a):
    high = a.astype(bf16)
    return high, (a - high.astype(f32)).astype(bf16)


def thirds(a):
    high = a.astype(bf16)
    rest = a - high.astype(f32)
    mid = rest.astype(bf16)
    return high, mid, (rest - mid.astype(f32)).astype(bf16)


def dot(a, b, dims):
    return lax.dot_general(a, b, dims, preferred_element_type=f32)


def dot3(a, b, dims):
    return dot(a[0], b[0], dims) + (dot(a[0], b[1], dims) + dot(a[1], b[0], dims))


def spread(cols, heads, width):
    row = lax.broadcasted_iota(jnp.int32, (3 * heads, width), 0)
    lane = lax.broadcasted_iota(jnp.int32, (3 * heads, width), 1)
    first = (row - jnp.where(row >= heads, heads, 0) - jnp.where(row >= 2 * heads, heads, 0)) * HEAD_SIZE
    pick = ((lane >= first) & (lane < first + HEAD_SIZE)).astype(f32).astype(bf16)
    parts = jnp.concatenate([p.astype(f32) for p in thirds(cols)], axis=1).astype(bf16)
    return dot(parts, pick, NN)


def segments(docs, first, length):
    count = docs.shape[1]
    up = lax.broadcasted_iota(jnp.int32, (count, count), 0)
    across = lax.broadcasted_iota(jnp.int32, (count, count), 1)
    start_col = jnp.sum(jnp.where(across < up, docs, 0.0), axis=1, keepdims=True)
    docs_col = jnp.sum(jnp.where(across == up, docs, 0.0), axis=1, keepdims=True)
    start_row = jnp.sum(jnp.where(up < across, docs_col, 0.0), axis=0, keepdims=True)
    at_col = (lax.broadcasted_iota(jnp.int32, (length, 1), 0) + first).astype(f32)
    at_row = (lax.broadcasted_iota(jnp.int32, (1, length), 1) + first).astype(f32)
    seg_col = jnp.sum(jnp.where(start_row <= at_col, 1.0, 0.0), axis=1, keepdims=True)
    seg_row = jnp.sum(jnp.where(start_col <= at_row, 1.0, 0.0), axis=0, keepdims=True)
    before = jnp.sum(jnp.where(start_row < first.astype(f32), 1.0, 0.0), axis=1, keepdims=True)
    return seg_col, seg_row, before


def head_row(ref, heads, width):
    lane = lax.broadcasted_iota(jnp.int32, (1, width), 1)
    out = jnp.zeros((1, width), f32)
    for h in range(heads):
        out = jnp.where((lane >= h * HEAD_SIZE) & (lane < (h + 1) * HEAD_SIZE), ref[h], out)
    return out


def edge_kernel(place, rates, docs, dt, x, g, b, c, send, keep, facts, segs, segr, last):
    length, width = x.shape
    heads = dt.shape[0]
    core = place[0] % 2
    first = place[0] * length
    seg_col, seg_row, before = segments(docs[...].astype(f32), first, length)
    seg_last = seg_col[length - 1 :, :]
    entry = (seg_col == before).astype(f32)
    final = (seg_col == seg_last).astype(f32)
    through = (seg_last == before).astype(f32)

    rate_col = jnp.zeros((heads, 1), f32)
    which = lax.broadcasted_iota(jnp.int32, (heads, 1), 0)
    for h in range(heads):
        rate_col = jnp.where(which == h, rates[h], rate_col)
    steps = dt[...]
    logs = -rate_col * steps
    t_at = lax.broadcasted_iota(jnp.int32, (length, length), 0)
    s_at = lax.broadcasted_iota(jnp.int32, (length, length), 1)
    lower = (s_at <= t_at).astype(f32).astype(bf16)
    eye = (s_at == t_at).astype(f32).astype(bf16)
    run = sum(dot(lower, p, NT) for p in thirds(logs))
    steps_t = sum(dot(eye, p, NT) for p in thirds(steps))
    grow = jnp.exp(run)
    shrink = jnp.exp(-run) * steps_t
    facts[...] = jnp.concatenate([grow, shrink], axis=1)
    col = lax.broadcasted_iota(jnp.int32, (length, 8), 1)
    segs[...] = jnp.where(col == 0, seg_col, jnp.where(col == 1, entry, final))
    segr[...] = jnp.broadcast_to(seg_row, (8, length))

    grow_x = spread(grow, heads, width)
    shrink_x = spread(shrink, heads, width)
    total = grow_x[length - 1 :, :]
    x_parts = halves(x[...] * shrink_x)
    g_parts = halves(g[...] * grow_x)
    is_zero = core == 0
    b_parts = halves((b[...] * final).T)
    c_parts = halves((c[...] * entry).T)
    end = dot3(b_parts, x_parts, NN) * total
    start = dot3(c_parts, g_parts, NN)
    last[...] = jnp.broadcast_to(total, (8, width))
    whole = jnp.broadcast_to(total * through, (8, width))
    send[:STATE, :] = jnp.where(is_zero, start, end)
    keep[:STATE, :] = jnp.where(is_zero, end, start)
    send[STATE:, :] = whole
    keep[STATE:, :] = whole


def local_kernel(place, skips, facts, segs, segr, x, g, b, c, y0, z0, mine, other, mh, ml, oh, ol):
    length, width = x.shape
    heads = facts.shape[1] // 2
    b_parts = halves(b[...])
    c_parts = halves(c[...])
    t_at = lax.broadcasted_iota(jnp.int32, (length, length), 0)
    s_at = lax.broadcasted_iota(jnp.int32, (length, length), 1)
    same = segs[:, :1] == segr[:1, :]
    mask = jnp.where(same & (s_at <= t_at), 1.0, 0.0)
    mask_t = jnp.where(same & (t_at <= s_at), 1.0, 0.0)
    core = place[0] % 2
    grow_x = spread(facts[:, :heads], heads, width)
    shrink_x = spread(facts[:, heads:], heads, width)
    x_parts = halves(x[...] * shrink_x)
    g_parts = halves(g[...] * grow_x)
    mh[...] = jnp.where(core == 0, g_parts[0], x_parts[0])
    ml[...] = jnp.where(core == 0, g_parts[1], x_parts[1])
    oh[...] = jnp.where(core == 0, x_parts[0], g_parts[0])
    ol[...] = jnp.where(core == 0, x_parts[1], g_parts[1])
    mix = halves(dot3(c_parts, b_parts, NT) * mask)
    mix_t = halves(dot3(b_parts, c_parts, NT) * mask_t)
    skip = head_row(skips, heads, width)
    y0[...] = dot3(mix, x_parts, NN) * grow_x + skip * x[...]
    z0[...] = dot3(mix_t, g_parts, NN) * shrink_x + skip * g[...]
    weight = dot3(g_parts, x_parts, NT) * mask
    grad_b = dot3(halves(weight.T), c_parts, NN)
    grad_c = dot3(halves(weight), b_parts, NN)
    mine[...] = jnp.where(core == 0, grad_c, grad_b)
    other[...] = jnp.where(core == 0, grad_b, grad_c)


def grad_kernel(core, place, state, last, segs, high, low, local, total):
    is_forward = place[0] % 2 == core
    scale = jnp.where(is_forward, 1.0, last[:1, :])
    tokens = jnp.where(is_forward, segs[:, 1:2], segs[:, 2:3])
    total[...] = local[...] + dot3((high[...], low[...]), halves(state[...] * scale), NT) * tokens


def out_kernel(place, mine, other, last, facts, segs, b, c, y0, z0, y, z):
    length, width = y0.shape
    heads = facts.shape[1] // 2
    is_zero = place[0] % 2 == 0
    mine_, other_ = mine[...], other[...]
    into = halves(jnp.where(is_zero, mine_, other_))
    after = halves(jnp.where(is_zero, other_, mine_) * last[:1, :])
    c_parts = halves(c[...] * segs[:, 1:2])
    b_parts = halves(b[...] * segs[:, 2:3])
    y[...] = (y0[...] + dot3(c_parts, into, NN) * spread(facts[:, :heads], heads, width)).astype(bf16)
    z[...] = (z0[...] + dot3(b_parts, after, NN) * spread(facts[:, heads:], heads, width)).astype(bf16)


def call(kernel, name, outs, smem, *args):
    specs = [pl.BlockSpec(memory_space=pltpu.SMEM if i in smem else pltpu.VMEM) for i in range(len(args))]
    return pl.pallas_call(
        kernel,
        name=name,
        out_shape=[jax.ShapeDtypeStruct(s, d) for s, d in outs],
        in_specs=specs,
        out_specs=[pl.BlockSpec(memory_space=pltpu.VMEM) for _ in outs],
    )(*args)


def build(seq, head):
    def route(a, target):
        pairs = []
        for s in range(seq):
            for h in range(head):
                s2, h2 = target(s, h)
                if 0 <= s2 < seq:
                    pairs.append((s * head + h, s2 * head + h2))
        return lax.ppermute(a, ("seq", "head"), pairs)

    def partner(a):
        return route(a, lambda s, h: (s ^ 1, h))

    def chips(a, hops):
        return route(a, lambda s, h: (s + 2 * hops if s % 2 == 0 else s - 2 * hops, h))

    def head_sum(a):
        a = a + route(a, lambda s, h: (s, h ^ 1 if s % 2 == 0 else h ^ 3))
        return a + route(a, lambda s, h: (s, h ^ 3 if s % 2 == 0 else h ^ 1))

    def body(x, b, c, dt, rates, skips, docs, g):
        length, width = x.shape
        heads = dt.shape[0]
        place = lax.axis_index("seq").astype(jnp.int32).reshape(1)
        state = (STATE + 8, width)
        wide = (length, width)
        send, keep, facts, segs, segr, last = call(
            edge_kernel, "edges",
            [(state, f32), (state, f32),
             ((length, 2 * heads), f32), ((length, 8), f32), ((8, length), f32), ((8, width), f32)],
            (0, 1), place, rates, docs.reshape(1, -1), dt, x, g, b, c)
        got = partner(send)
        row = lax.broadcasted_iota(jnp.int32, state, 0)
        chip = jnp.where(row < STATE, got, 0.0) + got[STATE : STATE + 1] * keep
        far = chips(chip, 2)
        near = chips(chip, 1)
        thin = ((length, STATE), f32)
        y0, z0, mine0, other0, mh, ml, oh, ol = call(
            local_kernel, "local", [(wide, f32), (wide, f32), thin, thin] + 4 * [(wide, bf16)],
            (0, 1), place, skips, facts, segs, segr, x, g, b, c)
        near, far, mine0 = lax.optimization_barrier((near, far, mine0))
        mine = near[:STATE] + near[STATE : STATE + 1] * far[:STATE]
        other = partner(keep[:STATE] + keep[STATE : STATE + 1] * mine)
        (first,) = call(partial(grad_kernel, 0), "first", [thin], (0,), place, mine, last, segs, mh, ml, mine0)
        (second,) = call(partial(grad_kernel, 1), "second", [thin], (0,), place, other, last, segs, oh, ol, other0)
        y, z = call(
            out_kernel, "outs", [(wide, bf16), (wide, bf16)],
            (0,), place, mine, other, last, facts, segs, b, c, y0, z0)
        first = head_sum(first)
        second = head_sum(second)
        zero = (place[0] & 1) == 0
        return y, z, jnp.where(zero, second, first), jnp.where(zero, first, second)

    return body


def solution(mesh):
    wide = P("seq", "head")
    row = P("seq", None)
    return jax.shard_map(
        build(mesh.shape["seq"], mesh.shape["head"]),
        mesh=mesh,
        in_specs=(wide, row, row, P("head", "seq"), P("head"), P("head"), P(), wide),
        out_specs=(wide, wide, row, row),
        check_vma=False,
    )
```
